512 devices in a mesh: uly: 8 (over x_hi, y), blk: 64 (over z, x_lo, core).
Axes of the slice: x: 4 (x_hi: 2, x_lo: 2; x = x_hi * 2 + x_lo), y: 4, z: 16, core: 2. Of those that a mesh axis runs over, the one named last changes fastest.
Arguments:
- query: bfloat16 [131072, 1024], P(('uly', 'blk')), as said below
- key: bfloat16 [131072, 1024], P(('uly', 'blk')), as said below
- value: bfloat16 [131072, 1024], P(('uly', 'blk')), may hold values from -5 to 5
- live: int32 [8, 16, 64, 27], P('uly', None, 'blk'), may hold values from 0 to 1, as said below
Outputs:
- attended: bfloat16 [131072, 1024], P(('uly', 'blk'))
The draws below stay inside these ranges and needn't reach their ends.
Inputs may be any that keep to these rules, and one draw needn't show every extreme that they name: `query`: entries lie within -5 to 5. `key`: entries lie within -5 to 5. live[h, f, s, 13] = 1 always; live is 0 for every neighbour that lies outside the grid of 16 x 8 x 8 tiles.
All inputs are finite; a program needn't handle non-finite values.
Results may differ from the reference program's by a relative error of at most 0.0046.
Values may be sent and summed in bfloat16 or wider, within the bound.
A program may use at most 128 MiB of HBM per device.

```python
import jax
import jax.numpy as jnp
from jax import lax

HD = 128
HEADS = 8
TILE = 128
TW = 8
TPD = 2
SPATIAL = 64
TH = 8
FRAMES = 16
TOKENS = 131072
N_ULY = 8
N_BLK = 64


def draw_query(key, part):
    own = jax.random.fold_in(key, 11)
    base = jnp.clip(jax.random.normal(own, (TOKENS, HEADS * HD), jnp.float32), -5.0, 5.0)
    return base.astype(jnp.bfloat16)


def draw_key(key, part):
    own = jax.random.fold_in(key, 12)
    base = jnp.clip(jax.random.normal(own, (TOKENS, HEADS * HD), jnp.float32), -5.0, 5.0)
    return base.astype(jnp.bfloat16)


def draw_live(key, part):
    own = jax.random.fold_in(key, 21)
    chance_key, roll_key, reach_key = jax.random.split(own, 3)
    chance = jax.random.randint(chance_key, (HEADS, 1, 1, 1), 30, 91)
    rolls = jax.random.randint(roll_key, (HEADS, FRAMES, SPATIAL, 27), 0, 100)
    reach = jax.random.randint(reach_key, (HEADS, 1, 1, 1), 0, 2)
    offsets = jnp.arange(27)
    frame_step = offsets // 9 - 1
    row_step = offsets // 3 % 3 - 1
    col_step = offsets % 3 - 1
    frames = jnp.arange(FRAMES)[:, None, None]
    spots = jnp.arange(SPATIAL)[None, :, None]
    heights = spots // TW + row_step
    widths = spots % TW + col_step
    inside = (frames + frame_step >= 0) & (frames + frame_step < FRAMES)
    inside = inside & (heights >= 0) & (heights < TH) & (widths >= 0) & (widths < TW)
    chosen = (rolls < chance) & (jnp.abs(frame_step) <= reach)
    keep = inside[None] & ((offsets == 13) | chosen)
    return keep.astype(jnp.int32)


def shard_levels(rng, shape, cuts, low, largest):
    loudness, own = 1.0, jax.random.fold_in(rng, 6)
    for axis_at, blocks in cuts:
        steps = jnp.exp(jax.random.uniform(jax.random.fold_in(own, axis_at), (blocks,), jnp.float32, low / len(cuts), largest / len(cuts)))
        loudness = loudness * jnp.repeat(steps, shape[axis_at] // blocks).reshape([-1 if axis == axis_at else 1 for axis in range(len(shape))])
    return loudness


def centred(key, shape, scale, bound, shards=(), held_as=jnp.bfloat16):
    loudness = shard_levels(key, shape, shards, -0.22, 0.18) if shards else 1.0
    values = jax.random.normal(key, shape, jnp.float32) * scale * loudness
    return jnp.minimum(jnp.maximum(values, -bound), bound).astype(held_as)


def setup_inputs(seed: int = 0) -> dict:
    arg_keys = jax.random.split(jax.random.key(seed), 5)
    return {
        "query": draw_query(jax.random.fold_in(arg_keys[4], 71), 0),
        "key": draw_key(jax.random.fold_in(arg_keys[4], 71), 0),
        "value": centred(arg_keys[2], (TOKENS, HEADS * HD), 1.0, 5.0, ((0, 512),)),
        "live": draw_live(jax.random.fold_in(arg_keys[4], 71), 0),
    }


def reference(query, key, value, live):
    scale = HD ** -0.5

    def tiles(tensor):
        shaped = tensor.reshape(N_ULY, N_BLK, TPD, TILE, HEADS, HD).transpose(4, 0, 2, 1, 3, 5)
        return shaped.reshape(HEADS, FRAMES, TH, TW, TILE, HD)

    grid_pad = ((1, 1), (1, 1), (1, 1), (0, 0), (0, 0))

    def one_head(inputs):
        query_head, key_head, value_head, live_head = inputs
        key_pad = jnp.pad(key_head, grid_pad)
        value_pad = jnp.pad(value_head, grid_pad)
        allowed_head = live_head.reshape(FRAMES, TH, TW, 27)

        def beside_all(block):
            parts = [block[frame_step, row_step:row_step + TH, col_step:col_step + TW]
                     for frame_step in range(3) for row_step in range(3) for col_step in range(3)]
            return jnp.stack(parts, axis=2)

        def one_frame(frame):
            key_near = beside_all(lax.dynamic_slice_in_dim(key_pad, frame, 3, 0)).astype(jnp.float32)
            value_near = beside_all(lax.dynamic_slice_in_dim(value_pad, frame, 3, 0)).astype(jnp.float32)
            query_frame = lax.dynamic_index_in_dim(query_head, frame, 0, keepdims=False).astype(jnp.float32)
            scores = jnp.einsum("abqd,abokd->abqok", query_frame, key_near,
                                precision=lax.Precision.HIGHEST) * scale
            allowed = (lax.dynamic_index_in_dim(allowed_head, frame, 0, keepdims=False) > 0)[:, :, None, :, None]
            masked = jnp.where(allowed, scores, -1e30)
            top = jnp.max(masked, axis=(3, 4), keepdims=True)
            weights = jnp.where(allowed, jnp.exp(masked - top), 0.0)
            total = jnp.sum(weights, axis=(3, 4))
            rounded = lax.optimization_barrier(weights.astype(jnp.bfloat16)).astype(jnp.float32)
            mixed = jnp.einsum("abqok,abokd->abqd", rounded, value_near,
                               precision=lax.Precision.HIGHEST)
            return (mixed / total[..., None]).astype(jnp.bfloat16)

        return lax.map(one_frame, jnp.arange(FRAMES))

    result = lax.map(one_head, (tiles(query), tiles(key), tiles(value), live))
    result = result.reshape(HEADS, N_ULY, TPD, N_BLK, TILE, HD).transpose(1, 3, 2, 4, 0, 5)
    return result.reshape(TOKENS, HEADS * HD)
```

```python
import math

import jax
import jax.numpy as jnp
from jax import lax
from jax.experimental import pallas as pl
from jax.experimental.pallas import tpu as pltpu
from jax.sharding import PartitionSpec as P

HD = 128
TILE = 128
TW = 8
TH = 8
N = 8
FRAMES = 2 * N
LAG_V = 1
LAG_H = 2
LOGIT = HD ** (-0.5) * math.log2(math.e)
NEG = -1e30
MESH = pl.DeviceIdType.MESH
DMA = pltpu.SemaphoreType.DMA


def kernel(
    q_hbm, k_hbm, v_hbm, live, out_hbm,
    kv, qb, ob, sc,
    a_send, a_recv, v_send, v_recv, h_send, h_recv, o_send, o_recv,
):
    u = lax.axis_index("uly")
    s = lax.axis_index("blk")
    h = s // TW
    w = s % TW
    up = ((h + 1) % TH) * TW + w
    down = ((h + TH - 1) % TH) * TW + w
    right = h * TW + (w + 1) % TW
    left = h * TW + (w + TW - 1) % TW
    has_up, has_down = h < TH - 1, h > 0
    has_right, has_left = w < TW - 1, w > 0
    has_row = (has_down, None, has_up)

    barrier = pltpu.get_barrier_semaphore()
    for i in range(1, N):
        pl.semaphore_signal(barrier, inc=1, device_id=((u + i) % N, s), device_id_type=MESH)
    for other in (up, down, left, right):
        pl.semaphore_signal(barrier, inc=1, device_id=(u, other), device_id_type=MESH)
    pl.semaphore_wait(barrier, N + 3)

    def columns(ref, head):
        return ref.at[:, pl.ds(pl.multiple_of(head * HD, HD), HD)]

    def a_dst(x, chunk):
        return qb.at[chunk] if x == 2 else kv.at[1, 1, chunk, x]

    def a_copy(x, to, chunk):
        ref = (k_hbm, v_hbm, q_hbm)[x]
        return pltpu.make_async_remote_copy(
            src_ref=columns(ref, to), dst_ref=a_dst(x, chunk),
            send_sem=a_send.at[x, to], recv_sem=a_recv.at[x, chunk],
            device_id=(to, s), device_id_type=MESH)

    def a_own(x):
        ref = (k_hbm, v_hbm, q_hbm)[x]
        return pltpu.make_async_copy(columns(ref, u), a_dst(x, u), a_recv.at[x, u])

    for x in (0, 1, 2):
        a_own(x).start()
    for xs in ((0, 1), (2,)):
        @pl.loop(1, N)
        def _(i):
            to = (u + N - i) % N
            for x in xs:
                a_copy(x, to, u).start()

    def v_copy(d, chunk):
        return pltpu.make_async_remote_copy(
            src_ref=kv.at[1, 1, chunk], dst_ref=kv.at[1, 0 if d == 0 else 2, chunk],
            send_sem=v_send.at[d, chunk], recv_sem=v_recv.at[d, chunk],
            device_id=(u, up if d == 0 else down), device_id_type=MESH)

    def h_copy(d, r, chunk):
        return pltpu.make_async_remote_copy(
            src_ref=kv.at[1, r, chunk], dst_ref=kv.at[0 if d == 0 else 2, r, chunk],
            send_sem=h_send.at[d, r, chunk], recv_sem=h_recv.at[d, r, chunk],
            device_id=(u, right if d == 0 else left), device_id_type=MESH)

    def o_dst(frame, head):
        return out_hbm.at[pl.ds(pl.multiple_of(frame % 2 * TILE, TILE), TILE),
                          pl.ds(pl.multiple_of(head * HD, HD), HD)]

    def o_copy(frame):
        return pltpu.make_async_remote_copy(
            src_ref=ob.at[frame], dst_ref=o_dst(frame, u),
            send_sem=o_send.at[frame], recv_sem=o_recv.at[u, frame % 2],
            device_id=(frame // 2, s), device_id_type=MESH)

    def o_own(frame):
        return pltpu.make_async_copy(ob.at[frame], o_dst(frame, u), o_send.at[frame])

    def zero(*at):
        @pl.loop(0, N)
        def _(g):
            for part in range(2):
                kv[(*at, g, part)] = jnp.zeros((2 * TILE, HD), jnp.bfloat16)

    for missing, spots in (
        (h == 0, [(c, 0) for c in range(3)]),
        (h == TH - 1, [(c, 2) for c in range(3)]),
        (w == 0, [(0, r) for r in range(3)]),
        (w == TW - 1, [(2, r) for r in range(3)]),
    ):
        @pl.when(missing)
        def _():
            for spot in spots:
                zero(*spot)

    def attend(f):
        q = qb[f // 2, pl.ds(pl.multiple_of(f % 2 * TILE, TILE), TILE), :]
        spots = []
        for a in range(3):
            g = (f + a + FRAMES - 1) % FRAMES
            spots.append((g // 2, pl.multiple_of(g % 2 * TILE, TILE)))

        def near(c, r, part):
            return jnp.concatenate(
                [kv[c, r, g, part, pl.ds(off, TILE), :] for g, off in spots], axis=0)

        top = jnp.full((TILE, TILE), NEG, jnp.float32)
        for r in range(3):
            for c in range(3):
                scores = lax.dot_general(
                    q, near(c, r, 0), (((1,), (1,)), ((), ())),
                    preferred_element_type=jnp.float32)
                for a in range(3):
                    bias = jnp.where(live[f * 27 + 9 * a + 3 * r + c] > 0, 0.0, NEG)
                    part = scores[:, a * TILE:(a + 1) * TILE] * LOGIT + bias
                    sc[3 * r + c, :, a * TILE:(a + 1) * TILE] = part
                    top = jnp.maximum(top, part)
        top = jnp.max(top, axis=1, keepdims=True)
        total = jnp.zeros((TILE, TILE), jnp.float32)
        mixed = jnp.zeros((TILE, HD), jnp.float32)
        for r in range(3):
            for c in range(3):
                weights = jnp.exp2(sc[3 * r + c] - top)
                for a in range(3):
                    total += weights[:, a * TILE:(a + 1) * TILE]
                mixed += jnp.dot(
                    weights.astype(jnp.bfloat16), near(c, r, 1),
                    preferred_element_type=jnp.float32)
        ob[f] = (mixed / jnp.sum(total, axis=1, keepdims=True)).astype(jnp.bfloat16)

    def attend_and_send(f):
        attend(f)

        @pl.when(f // 2 == u)
        def _():
            o_own(f).start()

        @pl.when(f // 2 != u)
        def _():
            o_copy(f).start()

    def unit(c):
        @pl.loop(0, 2)
        def _(j):
            attend_and_send((2 * c + j + FRAMES - 1) % FRAMES)

    def wait_a(x, chunk):
        pltpu.make_async_copy(columns(k_hbm, 0), a_dst(x, chunk), a_recv.at[x, chunk]).wait()

    @pl.loop(0, N + LAG_H)
    def _(i):
        @pl.when(i < N)
        def _():
            c = (u + i) % N
            wait_a(0, c)
            wait_a(1, c)

            @pl.when(has_up)
            def _():
                v_copy(0, c).start()

            @pl.when(has_down)
            def _():
                v_copy(1, c).start()

            @pl.when(has_right)
            def _():
                h_copy(0, 1, c).start()

            @pl.when(has_left)
            def _():
                h_copy(1, 1, c).start()

        @pl.when((i >= LAG_V) & (i < N + LAG_V))
        def _():
            c = (u + i + N - LAG_V) % N
            for d, r, there in ((0, 0, has_down), (1, 2, has_up)):
                @pl.when(there)
                def _():
                    v_copy(d, c).wait_recv()

                    @pl.when(has_right)
                    def _():
                        h_copy(0, r, c).start()

                    @pl.when(has_left)
                    def _():
                        h_copy(1, r, c).start()

        @pl.when(i >= LAG_H)
        def _():
            c = (u + i + N - LAG_H) % N
            for d, there in ((0, has_left), (1, has_right)):
                for r in range(3):
                    here = there if r == 1 else there & has_row[r]

                    @pl.when(here)
                    def _():
                        h_copy(d, r, c).wait_recv()
            wait_a(2, c)

            @pl.when(i > LAG_H)
            def _():
                unit(c)

    unit(u)

    @pl.loop(0, N)
    def _(g):
        @pl.when(has_up)
        def _():
            v_copy(0, g).wait_send()

        @pl.when(has_down)
        def _():
            v_copy(1, g).wait_send()

        for d, there in ((0, has_right), (1, has_left)):
            for r in range(3):
                here = there if r == 1 else there & has_row[r]

                @pl.when(here)
                def _():
                    h_copy(d, r, g).wait_send()

        @pl.when(g != u)
        def _():
            for x in range(3):
                a_copy(x, g, u).wait_send()
            for j in range(2):
                o_copy(2 * g + j).wait_send()
                pltpu.make_async_copy(ob.at[j], o_dst(j, g), o_recv.at[g, j]).wait()

        @pl.when(g == u)
        def _():
            for j in range(2):
                o_own(2 * g + j).wait()


def local(query, key, value, live):
    rows, width = query.shape
    hbm = pl.BlockSpec(memory_space=pl.ANY)
    return pl.pallas_call(
        kernel,
        out_shape=jax.ShapeDtypeStruct((rows, width), jnp.bfloat16),
        in_specs=[hbm, hbm, hbm, pl.BlockSpec(memory_space=pltpu.SMEM)],
        out_specs=hbm,
        scratch_shapes=[
            pltpu.VMEM((3, 3, N, 2, 2 * TILE, HD), jnp.bfloat16),
            pltpu.VMEM((N, 2 * TILE, HD), jnp.bfloat16),
            pltpu.VMEM((FRAMES, TILE, HD), jnp.bfloat16),
            pltpu.VMEM((9, TILE, 3 * TILE), jnp.float32),
            DMA((3, N)), DMA((3, N)),
            DMA((2, N)), DMA((2, N)),
            DMA((2, 3, N)), DMA((2, 3, N)),
            DMA((FRAMES,)), DMA((N, 2)),
        ],
        compiler_params=pltpu.CompilerParams(
            collective_id=0, has_side_effects=True, vmem_limit_bytes=48 << 20),
    )(query, key, value, live.reshape(-1))


def solution(mesh):
    return jax.shard_map(
        local,
        mesh=mesh,
        in_specs=(
            P(("uly", "blk"), None),
            P(("uly", "blk"), None),
            P(("uly", "blk"), None),
            P("uly", None, "blk", None),
        ),
        out_specs=P(("uly", "blk"), None),
        check_vma=False,
    )
```

```python
import functools
import math

import jax
import jax.numpy as jnp
from jax import lax
from jax.experimental import pallas as pl
from jax.experimental.pallas import tpu as pltpu
from jax.sharding import PartitionSpec as P

HD = 128
TILE = 128
TW = 8
TH = 8
N = 8
FRAMES = 2 * N
LAG_V = 1
LAG_R = 2
LAG_H = 3
LOGIT = HD ** (-0.5) * math.log2(math.e)
NEG = -1e30
MESH = pl.DeviceIdType.MESH
DMA = pltpu.SemaphoreType.DMA


def kernel(
    q_hbm, k_hbm, v_hbm, live, out_hbm,
    kv, qb, ob, sc, passing,
    a_send, a_recv, v_send, v_recv, h_send, h_recv, c_send, c_recv, r_send, r_recv, o_send, o_recv,
):
    u = lax.axis_index("uly")
    s = lax.axis_index("blk")
    h = s // TW
    w = s % TW
    up = ((h + 1) % TH) * TW + w
    down = ((h + TH - 1) % TH) * TW + w
    right = h * TW + (w + 1) % TW
    left = h * TW + (w + TW - 1) % TW
    has_up, has_down = h < TH - 1, h > 0
    has_right, has_left = w < TW - 1, w > 0
    has_row = (has_down, None, has_up)
    crosses = (w == 3) | (w == 4)
    relays = (w == 1) | (w == 6)
    relay = h * TW + jnp.where(w == 3, 1, 6)
    beyond = h * TW + jnp.where(w == 1, 4, 3)
    beyond_column = jnp.where(w == 1, 0, 2)
    far_column = jnp.where(w == 3, 2, 0)

    barrier = pltpu.get_barrier_semaphore()
    for i in range(1, N):
        pl.semaphore_signal(barrier, inc=1, device_id=((u + i) % N, s), device_id_type=MESH)
    for other in (up, down, left, right):
        pl.semaphore_signal(barrier, inc=1, device_id=(u, other), device_id_type=MESH)
    extra = crosses | relays

    @pl.when(extra)
    def _():
        for a, b in ((1, 3), (6, 4)):
            other = h * TW + jnp.where(crosses, a, b)
            pl.semaphore_signal(barrier, inc=1, device_id=(u, other), device_id_type=MESH)

    pl.semaphore_wait(barrier, N + 3 + 2 * extra.astype(jnp.int32))

    def columns(ref, head):
        return ref.at[:, pl.ds(pl.multiple_of(head * HD, HD), HD)]

    def a_dst(x, chunk):
        return qb.at[chunk] if x == 2 else kv.at[1, 1, chunk, x]

    def a_copy(x, to, chunk):
        ref = (k_hbm, v_hbm, q_hbm)[x]
        return pltpu.make_async_remote_copy(
            src_ref=columns(ref, to), dst_ref=a_dst(x, chunk),
            send_sem=a_send.at[x, to], recv_sem=a_recv.at[x, chunk],
            device_id=(to, s), device_id_type=MESH)

    def a_own(x):
        ref = (k_hbm, v_hbm, q_hbm)[x]
        return pltpu.make_async_copy(columns(ref, u), a_dst(x, u), a_recv.at[x, u])

    for x in (0, 1, 2):
        a_own(x).start()
    for xs in ((0, 1), (2,)):
        @pl.loop(1, N)
        def _(i):
            to = (u + N - i) % N
            for x in xs:
                a_copy(x, to, u).start()

    def v_copy(d, chunk):
        return pltpu.make_async_remote_copy(
            src_ref=kv.at[1, 1, chunk], dst_ref=kv.at[1, 0 if d == 0 else 2, chunk],
            send_sem=v_send.at[d, chunk], recv_sem=v_recv.at[d, chunk],
            device_id=(u, up if d == 0 else down), device_id_type=MESH)

    def h_copy(d, r, chunk):
        return pltpu.make_async_remote_copy(
            src_ref=kv.at[1, r, chunk], dst_ref=kv.at[0 if d == 0 else 2, r, chunk],
            send_sem=h_send.at[d, r, chunk], recv_sem=h_recv.at[d, r, chunk],
            device_id=(u, right if d == 0 else left), device_id_type=MESH)

    def near_half(d, r, chunk):
        return pltpu.make_async_remote_copy(
            src_ref=kv.at[1, r, chunk, 0], dst_ref=kv.at[0 if d == 0 else 2, r, chunk, 0],
            send_sem=h_send.at[d, r, chunk], recv_sem=h_recv.at[d, r, chunk],
            device_id=(u, right if d == 0 else left), device_id_type=MESH)

    def far_half(r, chunk):
        return pltpu.make_async_remote_copy(
            src_ref=kv.at[1, r, chunk, 1], dst_ref=passing.at[r, chunk],
            send_sem=c_send.at[r, chunk], recv_sem=r_recv.at[r, chunk],
            device_id=(u, relay), device_id_type=MESH)

    def forward(r, chunk):
        return pltpu.make_async_remote_copy(
            src_ref=passing.at[r, chunk], dst_ref=kv.at[beyond_column, r, chunk, 1],
            send_sem=r_send.at[r, chunk], recv_sem=c_recv.at[r, chunk],
            device_id=(u, beyond), device_id_type=MESH)

    def far_arrival(r, chunk):
        return pltpu.make_async_remote_copy(
            src_ref=passing.at[r, chunk], dst_ref=kv.at[far_column, r, chunk, 1],
            send_sem=r_send.at[r, chunk], recv_sem=c_recv.at[r, chunk],
            device_id=(u, beyond), device_id_type=MESH)

    def h_start(r, chunk):
        for d, there, wide in ((0, has_right, w == 3), (1, has_left, w == 4)):
            @pl.when(there & ~wide)
            def _():
                h_copy(d, r, chunk).start()

            @pl.when(wide)
            def _():
                far_half(r, chunk).start()
                near_half(d, r, chunk).start()

    def h_arrive(r, chunk):
        for d, there, wide in ((0, has_left, w == 4), (1, has_right, w == 3)):
            @pl.when(there & ~wide)
            def _():
                h_copy(d, r, chunk).wait_recv()

            @pl.when(wide)
            def _():
                near_half(d, r, chunk).wait_recv()
                far_arrival(r, chunk).wait_recv()

    def h_sent(r, chunk):
        for d, there, wide in ((0, has_right, w == 3), (1, has_left, w == 4)):
            @pl.when(there & ~wide)
            def _():
                h_copy(d, r, chunk).wait_send()

            @pl.when(wide)
            def _():
                far_half(r, chunk).wait_send()
                near_half(d, r, chunk).wait_send()

        @pl.when(relays)
        def _():
            forward(r, chunk).wait_send()

    def rows(action, chunk, which=(0, 1, 2)):
        for r in which:
            if r == 1:
                action(r, chunk)
            else:
                pl.when(has_row[r])(functools.partial(action, r, chunk))

    def pass_on(r, chunk):
        @pl.when(relays)
        def _():
            far_half(r, chunk).wait_recv()
            forward(r, chunk).start()

    def o_dst(frame, head):
        return out_hbm.at[pl.ds(pl.multiple_of(frame % 2 * TILE, TILE), TILE),
                          pl.ds(pl.multiple_of(head * HD, HD), HD)]

    def o_copy(frame):
        return pltpu.make_async_remote_copy(
            src_ref=ob.at[frame], dst_ref=o_dst(frame, u),
            send_sem=o_send.at[frame], recv_sem=o_recv.at[u, frame % 2],
            device_id=(frame // 2, s), device_id_type=MESH)

    def o_own(frame):
        return pltpu.make_async_copy(ob.at[frame], o_dst(frame, u), o_send.at[frame])

    def zero(*at):
        @pl.loop(0, N)
        def _(g):
            for part in range(2):
                kv[(*at, g, part)] = jnp.zeros((2 * TILE, HD), jnp.bfloat16)

    for missing, spots in (
        (h == 0, [(c, 0) for c in range(3)]),
        (h == TH - 1, [(c, 2) for c in range(3)]),
        (w == 0, [(0, r) for r in range(3)]),
        (w == TW - 1, [(2, r) for r in range(3)]),
    ):
        @pl.when(missing)
        def _():
            for spot in spots:
                zero(*spot)

    def attend(f):
        q = qb[f // 2, pl.ds(pl.multiple_of(f % 2 * TILE, TILE), TILE), :]
        spots = []
        for a in range(3):
            g = (f + a + FRAMES - 1) % FRAMES
            spots.append((g // 2, pl.multiple_of(g % 2 * TILE, TILE)))

        def near(c, r, part):
            return jnp.concatenate(
                [kv[c, r, g, part, pl.ds(off, TILE), :] for g, off in spots], axis=0)

        top = jnp.full((TILE, TILE), NEG, jnp.float32)
        for r in range(3):
            for c in range(3):
                scores = lax.dot_general(
                    q, near(c, r, 0), (((1,), (1,)), ((), ())),
                    preferred_element_type=jnp.float32)
                for a in range(3):
                    bias = jnp.where(live[0, f, 0, 9 * a + 3 * r + c] > 0, 0.0, NEG)
                    part = scores[:, a * TILE:(a + 1) * TILE] * LOGIT + bias
                    sc[3 * r + c, :, a * TILE:(a + 1) * TILE] = part
                    top = jnp.maximum(top, part)
        top = jnp.max(top, axis=1, keepdims=True)
        total = jnp.zeros((TILE, TILE), jnp.float32)
        mixed = jnp.zeros((TILE, HD), jnp.float32)
        for r in range(3):
            for c in range(3):
                weights = jnp.exp2(sc[3 * r + c] - top)
                for a in range(3):
                    total += weights[:, a * TILE:(a + 1) * TILE]
                mixed += jnp.dot(
                    weights.astype(jnp.bfloat16), near(c, r, 1),
                    preferred_element_type=jnp.float32)
        ob[f] = (mixed / jnp.sum(total, axis=1, keepdims=True)).astype(jnp.bfloat16)

    def attend_and_send(f):
        attend(f)

        @pl.when(f // 2 == u)
        def _():
            o_own(f).start()

        @pl.when(f // 2 != u)
        def _():
            o_copy(f).start()

    def unit(c):
        @pl.loop(0, 2)
        def _(j):
            attend_and_send((2 * c + j + FRAMES - 1) % FRAMES)

    def wait_a(x, chunk):
        pltpu.make_async_copy(columns(k_hbm, 0), a_dst(x, chunk), a_recv.at[x, chunk]).wait()

    @pl.loop(0, N + LAG_H)
    def _(i):
        @pl.when(i < N)
        def _():
            c = (u + i) % N
            wait_a(0, c)
            wait_a(1, c)

            @pl.when(has_up)
            def _():
                v_copy(0, c).start()

            @pl.when(has_down)
            def _():
                v_copy(1, c).start()

            h_start(1, c)

        @pl.when((i >= LAG_V) & (i < N + LAG_V))
        def _():
            c = (u + i + N - LAG_V) % N
            for d, r, there in ((0, 0, has_down), (1, 2, has_up)):
                @pl.when(there)
                def _():
                    v_copy(d, c).wait_recv()
                    h_start(r, c)

        @pl.when((i >= LAG_R) & (i < N + LAG_R))
        def _():
            rows(pass_on, (u + i + N - LAG_R) % N, (1, 0, 2))

        @pl.when(i >= LAG_H)
        def _():
            c = (u + i + N - LAG_H) % N
            rows(h_arrive, c)
            wait_a(2, c)

            @pl.when(i > LAG_H)
            def _():
                unit(c)

    unit(u)

    @pl.loop(0, N)
    def _(g):
        @pl.when(has_up)
        def _():
            v_copy(0, g).wait_send()

        @pl.when(has_down)
        def _():
            v_copy(1, g).wait_send()

        rows(h_sent, g)

        @pl.when(g != u)
        def _():
            for x in range(3):
                a_copy(x, g, u).wait_send()
            for j in range(2):
                o_copy(2 * g + j).wait_send()
                pltpu.make_async_copy(ob.at[j], o_dst(j, g), o_recv.at[g, j]).wait()

        @pl.when(g == u)
        def _():
            for j in range(2):
                o_own(2 * g + j).wait()


def local(query, key, value, live):
    rows, width = query.shape
    hbm = pl.BlockSpec(memory_space=pl.ANY)
    return pl.pallas_call(
        kernel,
        out_shape=jax.ShapeDtypeStruct((rows, width), jnp.bfloat16),
        in_specs=[hbm, hbm, hbm, pl.BlockSpec(memory_space=pltpu.SMEM)],
        out_specs=hbm,
        scratch_shapes=[
            pltpu.VMEM((3, 3, N, 2, 2 * TILE, HD), jnp.bfloat16),
            pltpu.VMEM((N, 2 * TILE, HD), jnp.bfloat16),
            pltpu.VMEM((FRAMES, TILE, HD), jnp.bfloat16),
            pltpu.VMEM((9, TILE, 3 * TILE), jnp.float32),
            pltpu.VMEM((3, N, 2 * TILE, HD), jnp.bfloat16),
            DMA((3, N)), DMA((3, N)),
            DMA((2, N)), DMA((2, N)),
            DMA((2, 3, N)), DMA((2, 3, N)),
            DMA((3, N)), DMA((3, N)), DMA((3, N)), DMA((3, N)),
            DMA((FRAMES,)), DMA((N, 2)),
        ],
        compiler_params=pltpu.CompilerParams(
            collective_id=0, has_side_effects=True, vmem_limit_bytes=62 << 20),
    )(query, key, value, live)


def solution(mesh):
    return jax.shard_map(
        local,
        mesh=mesh,
        in_specs=(
            P(("uly", "blk"), None),
            P(("uly", "blk"), None),
            P(("uly", "blk"), None),
            P("uly", None, "blk", None),
        ),
        out_specs=P(("uly", "blk"), None),
        check_vma=False,
    )
```

```python
import functools
import math

import jax
import jax.numpy as jnp
from jax import lax
from jax.experimental import pallas as pl
from jax.experimental.pallas import tpu as pltpu
from jax.sharding import PartitionSpec as P

HD = 128
TILE = 128
TW = 8
TH = 8
N = 8
FRAMES = 2 * N
LAG_V = 1
LAG_R = 2
LAG_H = 3
DIRECT = 2
LOGIT = HD ** (-0.5) * math.log2(math.e)
NEG = -1e30
MESH = pl.DeviceIdType.MESH
DMA = pltpu.SemaphoreType.DMA


def kernel(
    q_hbm, k_hbm, v_hbm, live_hbm, out_hbm,
    kv, qb, ob, sc, passing, live_in, live,
    a_send, a_recv, v_send, v_recv, h_send, h_recv, c_send, c_recv, r_send, r_recv, o_send, o_recv,
    l_send, l_recv,
):
    pu = lax.axis_index("uly")
    ps = lax.axis_index("blk")
    odd = ps // 4 % 2
    rx = (pu // 4 * 2 + ps // 2 % 2 + 4 - odd) % 4
    u = rx // 2 * 4 + pu % 4
    s = ps // 4 * 4 + rx % 2 * 2 + ps % 2
    even = odd == 0

    def place(head, tile):
        z = tile // 4
        x = (head // 4 * 2 + tile // 2 % 2 + z % 2) % 4
        return (x // 2 * 4 + head % 4, z * 4 + x % 2 * 2 + tile % 2)

    h = s // TW
    w = s % TW
    up = ((h + 1) % TH) * TW + w
    down = ((h + TH - 1) % TH) * TW + w
    right = h * TW + (w + 1) % TW
    left = h * TW + (w + TW - 1) % TW
    has_up, has_down = h < TH - 1, h > 0
    has_right, has_left = w < TW - 1, w > 0
    has_row = (has_down, None, has_up)
    crosses = (w == 3) | (w == 4)
    relays = (w == 1) | (w == 6)
    relay = h * TW + jnp.where(w == 3, 1, 6)
    beyond = h * TW + jnp.where(w == 1, 4, 3)
    beyond_column = jnp.where(w == 1, 0, 2)
    far_column = jnp.where(w == 3, 2, 0)

    extra = crosses | relays
    barrier = pltpu.get_barrier_semaphore()

    def greet(head, tile):
        pl.semaphore_signal(barrier, inc=1, device_id=place(head, tile), device_id_type=MESH)

    for i in range(1, N):
        greet((pu + i) % N, ps)
    for other in (up, down, left, right):
        greet(u, other)

    @pl.when(odd == 1)
    def _():
        greet(pu, ps)

    @pl.when(extra)
    def _():
        for a, b in ((1, 3), (6, 4)):
            other = h * TW + jnp.where(crosses, a, b)
            greet(u, other)
            greet((u + 4) % N, other)


    def columns(ref, head):
        return ref.at[:, pl.ds(pl.multiple_of(head * HD, HD), HD)]

    def a_dst(x, chunk):
        return qb.at[chunk] if x == 2 else kv.at[1, 1, chunk, x]

    def a_copy(x, to):
        ref = (k_hbm, v_hbm, q_hbm)[x]
        return pltpu.make_async_remote_copy(
            src_ref=columns(ref, to), dst_ref=a_dst(x, pu),
            send_sem=a_send.at[x, to], recv_sem=a_recv.at[x, pu],
            device_id=place(to, ps), device_id_type=MESH)

    def a_own(x):
        ref = (k_hbm, v_hbm, q_hbm)[x]
        return pltpu.make_async_copy(columns(ref, u), a_dst(x, u), a_recv.at[x, u])

    def live_copy():
        return pltpu.make_async_remote_copy(
            src_ref=live_hbm, dst_ref=live_in, send_sem=l_send, recv_sem=l_recv,
            device_id=place(pu, ps), device_id_type=MESH)

    def live_own():
        return pltpu.make_async_copy(live_hbm, live_in, l_recv)

    @pl.when(even)
    def _():
        for x in (0, 1, 2):
            a_own(x).start()
        live_own().start()

    def zero(*at):
        @pl.loop(0, N)
        def _(g):
            for part in range(2):
                kv[(*at, g, part)] = jnp.zeros((2 * TILE, HD), jnp.bfloat16)

    for missing, spots in (
        (h == 0, [(c, 0) for c in range(3)]),
        (h == TH - 1, [(c, 2) for c in range(3)]),
        (w == 0, [(0, r) for r in range(3)]),
        (w == TW - 1, [(2, r) for r in range(3)]),
    ):
        @pl.when(missing)
        def _():
            for spot in spots:
                zero(*spot)

    pl.semaphore_wait(barrier, N + 3 + odd + 4 * extra.astype(jnp.int32))

    @pl.when(odd == 1)
    def _():
        for x in (0, 1):
            a_copy(x, pu).start()

    for xs in ((0, 1), (2,)):
        @pl.loop(1, N)
        def _(i):
            to = (pu + N - i) % N
            for x in xs:
                a_copy(x, to).start()

    @pl.when(odd == 1)
    def _():
        a_copy(2, pu).start()
        live_copy().start()

    def v_copy(d, chunk):
        return pltpu.make_async_remote_copy(
            src_ref=kv.at[1, 1, chunk], dst_ref=kv.at[1, 0 if d == 0 else 2, chunk],
            send_sem=v_send.at[d, chunk], recv_sem=v_recv.at[d, chunk],
            device_id=place(u, up if d == 0 else down), device_id_type=MESH)

    def h_copy(d, r, chunk):
        return pltpu.make_async_remote_copy(
            src_ref=kv.at[1, r, chunk], dst_ref=kv.at[0 if d == 0 else 2, r, chunk],
            send_sem=h_send.at[d, r, chunk], recv_sem=h_recv.at[d, r, chunk],
            device_id=place(u, right if d == 0 else left), device_id_type=MESH)

    def near_half(d, r, chunk):
        return pltpu.make_async_remote_copy(
            src_ref=kv.at[1, r, chunk, 0], dst_ref=kv.at[0 if d == 0 else 2, r, chunk, 0],
            send_sem=h_send.at[d, r, chunk], recv_sem=h_recv.at[d, r, chunk],
            device_id=place(u, right if d == 0 else left), device_id_type=MESH)

    def via(chunk):
        return jnp.where(chunk % 2 == 0, u, (u + 4) % N)

    def far_half(r, chunk):
        return pltpu.make_async_remote_copy(
            src_ref=kv.at[1, r, chunk, 1], dst_ref=passing.at[r, chunk],
            send_sem=c_send.at[r, chunk], recv_sem=r_recv.at[r, chunk],
            device_id=place(via(chunk), relay), device_id_type=MESH)

    def forward(r, chunk):
        return pltpu.make_async_remote_copy(
            src_ref=passing.at[r, chunk], dst_ref=kv.at[beyond_column, r, chunk, 1],
            send_sem=r_send.at[r, chunk], recv_sem=c_recv.at[r, chunk],
            device_id=place(via(chunk), beyond), device_id_type=MESH)

    def far_arrival(r, chunk):
        return pltpu.make_async_remote_copy(
            src_ref=passing.at[r, chunk], dst_ref=kv.at[far_column, r, chunk, 1],
            send_sem=r_send.at[r, chunk], recv_sem=c_recv.at[r, chunk],
            device_id=place(via(chunk), beyond), device_id_type=MESH)

    def late(chunk):
        return (chunk + N - u) % N >= N - DIRECT

    def late_by(chunk):
        return (chunk + N - via(chunk)) % N >= N - DIRECT

    def h_start(r, chunk):
        for d, there, wide in ((0, has_right, (w == 3) & ~late(chunk)), (1, has_left, (w == 4) & ~late(chunk))):
            @pl.when(there & ~wide)
            def _():
                h_copy(d, r, chunk).start()

            @pl.when(wide)
            def _():
                far_half(r, chunk).start()
                near_half(d, r, chunk).start()

    def h_arrive(r, chunk):
        for d, there, wide in ((0, has_left, (w == 4) & ~late(chunk)), (1, has_right, (w == 3) & ~late(chunk))):
            @pl.when(there & ~wide)
            def _():
                h_copy(d, r, chunk).wait_recv()

            @pl.when(wide)
            def _():
                near_half(d, r, chunk).wait_recv()
                far_arrival(r, chunk).wait_recv()

    def h_sent(r, chunk):
        for d, there, wide in ((0, has_right, (w == 3) & ~late(chunk)), (1, has_left, (w == 4) & ~late(chunk))):
            @pl.when(there & ~wide)
            def _():
                h_copy(d, r, chunk).wait_send()

            @pl.when(wide)
            def _():
                far_half(r, chunk).wait_send()
                near_half(d, r, chunk).wait_send()

        @pl.when(relays & ~late_by(chunk))
        def _():
            forward(r, chunk).wait_send()

    def rows(action, chunk, which=(0, 1, 2)):
        for r in which:
            if r == 1:
                action(r, chunk)
            else:
                pl.when(has_row[r])(functools.partial(action, r, chunk))

    def pass_on(r, chunk):
        @pl.when(relays & ~late_by(chunk))
        def _():
            far_half(r, chunk).wait_recv()
            forward(r, chunk).start()

    def o_dst(frame, head):
        return out_hbm.at[pl.ds(pl.multiple_of(frame % 2 * TILE, TILE), TILE),
                          pl.ds(pl.multiple_of(head * HD, HD), HD)]

    def o_copy(frame):
        return pltpu.make_async_remote_copy(
            src_ref=ob.at[frame], dst_ref=o_dst(frame, u),
            send_sem=o_send.at[frame], recv_sem=o_recv.at[u, frame % 2],
            device_id=(frame // 2, s), device_id_type=MESH)

    def o_own(frame):
        return pltpu.make_async_copy(ob.at[frame], o_dst(frame, u), o_send.at[frame])

    def attend(f):
        q = qb[f // 2, pl.ds(pl.multiple_of(f % 2 * TILE, TILE), TILE), :]
        spots = []
        for a in range(3):
            g = (f + a + FRAMES - 1) % FRAMES
            spots.append((g // 2, pl.multiple_of(g % 2 * TILE, TILE)))

        def near(c, r, part):
            return jnp.concatenate(
                [kv[c, r, g, part, pl.ds(off, TILE), :] for g, off in spots], axis=0)

        top = jnp.full((TILE, TILE), NEG, jnp.float32)
        for r in range(3):
            for c in range(3):
                scores = lax.dot_general(
                    q, near(c, r, 0), (((1,), (1,)), ((), ())),
                    preferred_element_type=jnp.float32)
                for a in range(3):
                    bias = jnp.where(live[0, f, 0, 9 * a + 3 * r + c] > 0, 0.0, NEG)
                    part = scores[:, a * TILE:(a + 1) * TILE] * LOGIT + bias
                    sc[3 * r + c, :, a * TILE:(a + 1) * TILE] = part
                    top = jnp.maximum(top, part)
        top = jnp.max(top, axis=1, keepdims=True)
        total = jnp.zeros((TILE, TILE), jnp.float32)
        mixed = jnp.zeros((TILE, HD), jnp.float32)
        for r in range(3):
            for c in range(3):
                weights = jnp.exp2(sc[3 * r + c] - top)
                for a in range(3):
                    total += weights[:, a * TILE:(a + 1) * TILE]
                mixed += jnp.dot(
                    weights.astype(jnp.bfloat16), near(c, r, 1),
                    preferred_element_type=jnp.float32)
        ob[f] = (mixed / jnp.sum(total, axis=1, keepdims=True)).astype(jnp.bfloat16)

    def attend_and_send(f):
        attend(f)

        @pl.when(even & (f // 2 == u))
        def _():
            o_own(f).start()

        @pl.when((odd == 1) | (f // 2 != u))
        def _():
            o_copy(f).start()

    def unit(c):
        @pl.loop(0, 2)
        def _(j):
            attend_and_send((2 * c + j + FRAMES - 1) % FRAMES)

    def wait_a(x, chunk):
        pltpu.make_async_copy(columns(k_hbm, 0), a_dst(x, chunk), a_recv.at[x, chunk]).wait()

    @pl.loop(0, N + LAG_H)
    def _(i):
        @pl.when(i < N)
        def _():
            c = (u + i) % N
            wait_a(0, c)
            wait_a(1, c)

            @pl.when(has_up)
            def _():
                v_copy(0, c).start()

            @pl.when(has_down)
            def _():
                v_copy(1, c).start()

            h_start(1, c)

        @pl.when((i >= LAG_V) & (i < N + LAG_V))
        def _():
            c = (u + i + N - LAG_V) % N
            for d, r, there in ((0, 0, has_down), (1, 2, has_up)):
                @pl.when(there)
                def _():
                    v_copy(d, c).wait_recv()
                    h_start(r, c)

        @pl.when((i >= LAG_R) & (i < N + LAG_R))
        def _():
            c = (u + i + N - LAG_R) % N
            rows(pass_on, jnp.where(c % 2 == 0, c, (c + 4) % N), (1, 0, 2))

        @pl.when(i == LAG_H)
        def _():
            live_own().wait()
            pltpu.sync_copy(live_in, live)

        @pl.when(i >= LAG_H)
        def _():
            c = (u + i + N - LAG_H) % N
            rows(h_arrive, c)
            wait_a(2, c)

            @pl.when(i > LAG_H)
            def _():
                unit(c)

    unit(u)

    @pl.when(odd == 1)
    def _():
        live_copy().wait_send()

    @pl.loop(0, N)
    def _(g):
        @pl.when(has_up)
        def _():
            v_copy(0, g).wait_send()

        @pl.when(has_down)
        def _():
            v_copy(1, g).wait_send()

        rows(h_sent, g)

        @pl.when((odd == 1) | (g != u))
        def _():
            for x in range(3):
                a_copy(x, g).wait_send()
            for j in range(2):
                o_copy(2 * g + j).wait_send()
                pltpu.make_async_copy(ob.at[j], o_dst(j, g), o_recv.at[g, j]).wait()

        @pl.when(even & (g == u))
        def _():
            for j in range(2):
                o_own(2 * g + j).wait()


def local(query, key, value, live):
    rows, width = query.shape
    hbm = pl.BlockSpec(memory_space=pl.ANY)
    return pl.pallas_call(
        kernel,
        out_shape=jax.ShapeDtypeStruct((rows, width), jnp.bfloat16),
        in_specs=[hbm] * 4,
        out_specs=hbm,
        scratch_shapes=[
            pltpu.VMEM((3, 3, N, 2, 2 * TILE, HD), jnp.bfloat16),
            pltpu.VMEM((N, 2 * TILE, HD), jnp.bfloat16),
            pltpu.VMEM((FRAMES, TILE, HD), jnp.bfloat16),
            pltpu.VMEM((9, TILE, 3 * TILE), jnp.float32),
            pltpu.VMEM((3, N, 2 * TILE, HD), jnp.bfloat16),
            pltpu.VMEM(live.shape, jnp.int32), pltpu.SMEM(live.shape, jnp.int32),
            DMA((3, N)), DMA((3, N)),
            DMA((2, N)), DMA((2, N)),
            DMA((2, 3, N)), DMA((2, 3, N)),
            DMA((3, N)), DMA((3, N)), DMA((3, N)), DMA((3, N)),
            DMA((FRAMES,)), DMA((N, 2)),
            DMA, DMA,
        ],
        compiler_params=pltpu.CompilerParams(
            collective_id=0, has_side_effects=True, vmem_limit_bytes=53 << 20),
    )(query, key, value, live)


def solution(mesh):
    return jax.shard_map(
        local,
        mesh=mesh,
        in_specs=(
            P(("uly", "blk"), None),
            P(("uly", "blk"), None),
            P(("uly", "blk"), None),
            P("uly", None, "blk", None),
        ),
        out_specs=P(("uly", "blk"), None),
        check_vma=False,
    )
```

```python
import functools
import math

import jax
import jax.numpy as jnp
from jax import lax
from jax.experimental import pallas as pl
from jax.experimental.pallas import tpu as pltpu
from jax.sharding import PartitionSpec as P

HD = 128
TILE = 128
TW = 8
TH = 8
N = 8
FRAMES = 2 * N
LAG_V = 2
LAG_R = 3
LAG_H = 4
DIRECT = 2
LOGIT = HD ** (-0.5) * math.log2(math.e)
NEG = -1e30
MESH = pl.DeviceIdType.MESH
DMA = pltpu.SemaphoreType.DMA


def kernel(
    q_hbm, k_hbm, v_hbm, live_hbm, out_hbm,
    kv, qb, ob, sc, passing, live_in, live,
    a_send, a_recv, v_send, v_recv, h_send, h_recv, c_send, c_recv, r_send, r_recv, o_send, o_recv,
    l_send, l_recv,
):
    pu = lax.axis_index("uly")
    ps = lax.axis_index("blk")
    odd = ps // 4 % 2
    rx = (pu // 4 * 2 + ps // 2 % 2 + 4 - odd) % 4
    u = rx // 2 * 4 + pu % 4
    s = ps // 4 * 4 + rx % 2 * 2 + ps % 2
    even = odd == 0

    def place(head, tile):
        z = tile // 4
        x = (head // 4 * 2 + tile // 2 % 2 + z % 2) % 4
        return (x // 2 * 4 + head % 4, z * 4 + x % 2 * 2 + tile % 2)

    h = s // TW
    w = s % TW
    up = ((h + 1) % TH) * TW + w
    down = ((h + TH - 1) % TH) * TW + w
    right = h * TW + (w + 1) % TW
    left = h * TW + (w + TW - 1) % TW
    has_up, has_down = h < TH - 1, h > 0
    has_right, has_left = w < TW - 1, w > 0
    has_row = (has_down, None, has_up)
    crosses = (w == 3) | (w == 4)
    relays = (w == 1) | (w == 6)
    relay = h * TW + jnp.where(w == 3, 1, 6)
    beyond = h * TW + jnp.where(w == 1, 4, 3)
    beyond_column = jnp.where(w == 1, 0, 2)
    far_column = jnp.where(w == 3, 2, 0)

    extra = crosses | relays
    barrier = pltpu.get_barrier_semaphore()

    def greet(head, tile):
        pl.semaphore_signal(barrier, inc=1, device_id=place(head, tile), device_id_type=MESH)

    for i in range(1, N):
        greet((pu + i) % N, ps)
    for other in (up, down, left, right):
        greet(u, other)

    @pl.when(odd == 1)
    def _():
        greet(pu, ps)

    @pl.when(extra)
    def _():
        for a, b in ((1, 3), (6, 4)):
            other = h * TW + jnp.where(crosses, a, b)
            greet(u, other)
            greet((u + 4) % N, other)


    def columns(ref, head):
        return ref.at[:, pl.ds(pl.multiple_of(head * HD, HD), HD)]

    def a_dst(x, chunk):
        return qb.at[chunk] if x == 2 else kv.at[1, 1, chunk, x]

    def a_copy(x, to):
        ref = (k_hbm, v_hbm, q_hbm)[x]
        return pltpu.make_async_remote_copy(
            src_ref=columns(ref, to), dst_ref=a_dst(x, pu),
            send_sem=a_send.at[x, to], recv_sem=a_recv.at[x, pu],
            device_id=place(to, ps), device_id_type=MESH)

    def a_own(x):
        ref = (k_hbm, v_hbm, q_hbm)[x]
        return pltpu.make_async_copy(columns(ref, u), a_dst(x, u), a_recv.at[x, u])

    def live_copy():
        return pltpu.make_async_remote_copy(
            src_ref=live_hbm, dst_ref=live_in, send_sem=l_send, recv_sem=l_recv,
            device_id=place(pu, ps), device_id_type=MESH)

    def live_own():
        return pltpu.make_async_copy(live_hbm, live_in, l_recv)

    @pl.when(even)
    def _():
        for x in (0, 1, 2):
            a_own(x).start()
        live_own().start()

    def zero(*at):
        @pl.loop(0, N)
        def _(g):
            for part in range(2):
                kv[(*at, g, part)] = jnp.zeros((2 * TILE, HD), jnp.bfloat16)

    for missing, spots in (
        (h == 0, [(c, 0) for c in range(3)]),
        (h == TH - 1, [(c, 2) for c in range(3)]),
        (w == 0, [(0, r) for r in range(3)]),
        (w == TW - 1, [(2, r) for r in range(3)]),
    ):
        @pl.when(missing)
        def _():
            for spot in spots:
                zero(*spot)

    pl.semaphore_wait(barrier, N + 3 + odd + 4 * extra.astype(jnp.int32))

    @pl.when(odd == 1)
    def _():
        for x in (0, 1):
            a_copy(x, pu).start()

    for xs in ((0, 1), (2,)):
        @pl.loop(1, N)
        def _(i):
            to = (pu + N - i) % N
            for x in xs:
                a_copy(x, to).start()

    @pl.when(odd == 1)
    def _():
        a_copy(2, pu).start()
        live_copy().start()

    def v_copy(d, chunk):
        return pltpu.make_async_remote_copy(
            src_ref=kv.at[1, 1, chunk], dst_ref=kv.at[1, 0 if d == 0 else 2, chunk],
            send_sem=v_send.at[d, chunk], recv_sem=v_recv.at[d, chunk],
            device_id=place(u, up if d == 0 else down), device_id_type=MESH)

    def h_copy(d, r, chunk):
        return pltpu.make_async_remote_copy(
            src_ref=kv.at[1, r, chunk], dst_ref=kv.at[0 if d == 0 else 2, r, chunk],
            send_sem=h_send.at[d, r, chunk], recv_sem=h_recv.at[d, r, chunk],
            device_id=place(u, right if d == 0 else left), device_id_type=MESH)

    def near_half(d, r, chunk):
        return pltpu.make_async_remote_copy(
            src_ref=kv.at[1, r, chunk, 0], dst_ref=kv.at[0 if d == 0 else 2, r, chunk, 0],
            send_sem=h_send.at[d, r, chunk], recv_sem=h_recv.at[d, r, chunk],
            device_id=place(u, right if d == 0 else left), device_id_type=MESH)

    def via(chunk):
        return jnp.where(chunk % 2 == 0, u, (u + 4) % N)

    def far_half(r, chunk):
        return pltpu.make_async_remote_copy(
            src_ref=kv.at[1, r, chunk, 1], dst_ref=passing.at[r, chunk],
            send_sem=c_send.at[r, chunk], recv_sem=r_recv.at[r, chunk],
            device_id=place(via(chunk), relay), device_id_type=MESH)

    def forward(r, chunk):
        return pltpu.make_async_remote_copy(
            src_ref=passing.at[r, chunk], dst_ref=kv.at[beyond_column, r, chunk, 1],
            send_sem=r_send.at[r, chunk], recv_sem=c_recv.at[r, chunk],
            device_id=place(via(chunk), beyond), device_id_type=MESH)

    def far_arrival(r, chunk):
        return pltpu.make_async_remote_copy(
            src_ref=passing.at[r, chunk], dst_ref=kv.at[far_column, r, chunk, 1],
            send_sem=r_send.at[r, chunk], recv_sem=c_recv.at[r, chunk],
            device_id=place(via(chunk), beyond), device_id_type=MESH)

    def late(chunk):
        return (chunk + N - u) % N >= N - DIRECT

    def late_by(chunk):
        return (chunk + N - via(chunk)) % N >= N - DIRECT

    def h_start(r, chunk):
        for d, there, wide in ((0, has_right, (w == 3) & ~late(chunk)), (1, has_left, (w == 4) & ~late(chunk))):
            @pl.when(there & ~wide)
            def _():
                h_copy(d, r, chunk).start()

            @pl.when(wide)
            def _():
                far_half(r, chunk).start()
                near_half(d, r, chunk).start()

    def h_arrive(r, chunk):
        for d, there, wide in ((0, has_left, (w == 4) & ~late(chunk)), (1, has_right, (w == 3) & ~late(chunk))):
            @pl.when(there & ~wide)
            def _():
                h_copy(d, r, chunk).wait_recv()

            @pl.when(wide)
            def _():
                near_half(d, r, chunk).wait_recv()
                far_arrival(r, chunk).wait_recv()

    def h_sent(r, chunk):
        for d, there, wide in ((0, has_right, (w == 3) & ~late(chunk)), (1, has_left, (w == 4) & ~late(chunk))):
            @pl.when(there & ~wide)
            def _():
                h_copy(d, r, chunk).wait_send()

            @pl.when(wide)
            def _():
                far_half(r, chunk).wait_send()
                near_half(d, r, chunk).wait_send()

        @pl.when(relays & ~late_by(chunk))
        def _():
            forward(r, chunk).wait_send()

    def rows(action, chunk, which=(0, 1, 2)):
        for r in which:
            if r == 1:
                action(r, chunk)
            else:
                pl.when(has_row[r])(functools.partial(action, r, chunk))

    def pass_on(r, chunk):
        @pl.when(relays & ~late_by(chunk))
        def _():
            far_half(r, chunk).wait_recv()
            forward(r, chunk).start()

    def o_dst(frame, head):
        return out_hbm.at[pl.ds(pl.multiple_of(frame % 2 * TILE, TILE), TILE),
                          pl.ds(pl.multiple_of(head * HD, HD), HD)]

    def o_copy(frame):
        return pltpu.make_async_remote_copy(
            src_ref=ob.at[frame], dst_ref=o_dst(frame, u),
            send_sem=o_send.at[frame], recv_sem=o_recv.at[u, frame % 2],
            device_id=(frame // 2, s), device_id_type=MESH)

    def o_own(frame):
        return pltpu.make_async_copy(ob.at[frame], o_dst(frame, u), o_send.at[frame])

    def attend(f):
        q = qb[f // 2, pl.ds(pl.multiple_of(f % 2 * TILE, TILE), TILE), :]
        spots = []
        for a in range(3):
            g = (f + a + FRAMES - 1) % FRAMES
            spots.append((g // 2, pl.multiple_of(g % 2 * TILE, TILE)))

        def near(c, r, part):
            return jnp.concatenate(
                [kv[c, r, g, part, pl.ds(off, TILE), :] for g, off in spots], axis=0)

        top = jnp.full((TILE, TILE), NEG, jnp.float32)
        for r in range(3):
            for c in range(3):
                scores = lax.dot_general(
                    q, near(c, r, 0), (((1,), (1,)), ((), ())),
                    preferred_element_type=jnp.float32)
                for a in range(3):
                    bias = jnp.where(live[0, f, 0, 9 * a + 3 * r + c] > 0, 0.0, NEG)
                    part = scores[:, a * TILE:(a + 1) * TILE] * LOGIT + bias
                    sc[3 * r + c, :, a * TILE:(a + 1) * TILE] = part
                    top = jnp.maximum(top, part)
        top = jnp.max(top, axis=1, keepdims=True)
        total = jnp.zeros((TILE, TILE), jnp.float32)
        mixed = jnp.zeros((TILE, HD), jnp.float32)
        for r in range(3):
            for c in range(3):
                weights = jnp.exp2(sc[3 * r + c] - top)
                for a in range(3):
                    total += weights[:, a * TILE:(a + 1) * TILE]
                mixed += jnp.dot(
                    weights.astype(jnp.bfloat16), near(c, r, 1),
                    preferred_element_type=jnp.float32)
        ob[f] = (mixed / jnp.sum(total, axis=1, keepdims=True)).astype(jnp.bfloat16)

    def attend_and_send(f):
        attend(f)

        @pl.when(even & (f // 2 == u))
        def _():
            o_own(f).start()

        @pl.when((odd == 1) | (f // 2 != u))
        def _():
            o_copy(f).start()

    def unit(c):
        @pl.loop(0, 2)
        def _(j):
            attend_and_send((2 * c + j + FRAMES - 1) % FRAMES)

    def wait_a(x, chunk):
        pltpu.make_async_copy(columns(k_hbm, 0), a_dst(x, chunk), a_recv.at[x, chunk]).wait()

    @pl.loop(0, N + LAG_H)
    def _(i):
        @pl.when(i < N)
        def _():
            c = (u + i) % N
            wait_a(0, c)
            wait_a(1, c)

            @pl.when(has_up)
            def _():
                v_copy(0, c).start()

            @pl.when(has_down)
            def _():
                v_copy(1, c).start()

            h_start(1, c)

        @pl.when((i >= LAG_V) & (i < N + LAG_V))
        def _():
            c = (u + i + N - LAG_V) % N
            for d, r, there in ((0, 0, has_down), (1, 2, has_up)):
                @pl.when(there)
                def _():
                    v_copy(d, c).wait_recv()
                    h_start(r, c)

        @pl.when((i >= LAG_R) & (i < N + LAG_R))
        def _():
            c = (u + i + N - LAG_R) % N
            rows(pass_on, jnp.where(c % 2 == 0, c, (c + 4) % N), (1, 0, 2))

        @pl.when(i == LAG_H)
        def _():
            live_own().wait()
            pltpu.sync_copy(live_in, live)

        @pl.when(i >= LAG_H)
        def _():
            c = (u + i + N - LAG_H) % N
            rows(h_arrive, c)
            wait_a(2, c)

            @pl.when(i > LAG_H)
            def _():
                unit(c)

    unit(u)

    @pl.when(odd == 1)
    def _():
        live_copy().wait_send()

    @pl.loop(0, N)
    def _(g):
        @pl.when(has_up)
        def _():
            v_copy(0, g).wait_send()

        @pl.when(has_down)
        def _():
            v_copy(1, g).wait_send()

        rows(h_sent, g)

        @pl.when((odd == 1) | (g != u))
        def _():
            for x in range(3):
                a_copy(x, g).wait_send()
            for j in range(2):
                o_copy(2 * g + j).wait_send()
                pltpu.make_async_copy(ob.at[j], o_dst(j, g), o_recv.at[g, j]).wait()

        @pl.when(even & (g == u))
        def _():
            for j in range(2):
                o_own(2 * g + j).wait()


def local(query, key, value, live):
    rows, width = query.shape
    hbm = pl.BlockSpec(memory_space=pl.ANY)
    return pl.pallas_call(
        kernel,
        out_shape=jax.ShapeDtypeStruct((rows, width), jnp.bfloat16),
        in_specs=[hbm] * 4,
        out_specs=hbm,
        scratch_shapes=[
            pltpu.VMEM((3, 3, N, 2, 2 * TILE, HD), jnp.bfloat16),
            pltpu.VMEM((N, 2 * TILE, HD), jnp.bfloat16),
            pltpu.VMEM((FRAMES, TILE, HD), jnp.bfloat16),
            pltpu.VMEM((9, TILE, 3 * TILE), jnp.float32),
            pltpu.VMEM((3, N, 2 * TILE, HD), jnp.bfloat16),
            pltpu.VMEM(live.shape, jnp.int32), pltpu.SMEM(live.shape, jnp.int32),
            DMA((3, N)), DMA((3, N)),
            DMA((2, N)), DMA((2, N)),
            DMA((2, 3, N)), DMA((2, 3, N)),
            DMA((3, N)), DMA((3, N)), DMA((3, N)), DMA((3, N)),
            DMA((FRAMES,)), DMA((N, 2)),
            DMA, DMA,
        ],
        compiler_params=pltpu.CompilerParams(
            collective_id=0, has_side_effects=True, vmem_limit_bytes=53 << 20),
    )(query, key, value, live)


def solution(mesh):
    return jax.shard_map(
        local,
        mesh=mesh,
        in_specs=(
            P(("uly", "blk"), None),
            P(("uly", "blk"), None),
            P(("uly", "blk"), None),
            P("uly", None, "blk", None),
        ),
        out_specs=P(("uly", "blk"), None),
        check_vma=False,
    )
```

```python
import functools
import math

import jax
import jax.numpy as jnp
from jax import lax
from jax.experimental import pallas as pl
from jax.experimental.pallas import tpu as pltpu
from jax.sharding import PartitionSpec as P

HD = 128
TILE = 128
TW = 8
TH = 8
N = 8
FRAMES = 2 * N
LAG_V = 1
LAG_R = 2
LAG_H = 3
DIRECT = 2
LOGIT = HD ** (-0.5) * math.log2(math.e)
NEG = -1e30
MESH = pl.DeviceIdType.MESH
DMA = pltpu.SemaphoreType.DMA


def kernel(
    q_hbm, k_hbm, v_hbm, live_hbm, out_hbm,
    kv, qb, ob, sc, passing, live_in, live,
    a_send, a_recv, v_send, v_recv, h_send, h_recv, c_send, c_recv, r_send, r_recv, o_send, o_recv,
    l_send, l_recv,
):
    pu = lax.axis_index("uly")
    ps = lax.axis_index("blk")
    odd = ps // 4 % 2
    rx = (pu // 4 * 2 + ps // 2 % 2 + 4 - odd) % 4
    u = rx // 2 * 4 + pu % 4
    s = ps // 4 * 4 + rx % 2 * 2 + ps % 2
    even = odd == 0

    def place(head, tile):
        z = tile // 4
        x = (head // 4 * 2 + tile // 2 % 2 + z % 2) % 4
        return (x // 2 * 4 + head % 4, z * 4 + x % 2 * 2 + tile % 2)

    h = s // TW
    w = s % TW
    up = ((h + 1) % TH) * TW + w
    down = ((h + TH - 1) % TH) * TW + w
    right = h * TW + (w + 1) % TW
    left = h * TW + (w + TW - 1) % TW
    has_up, has_down = h < TH - 1, h > 0
    has_right, has_left = w < TW - 1, w > 0
    has_row = (has_down, None, has_up)
    crosses = (w == 3) | (w == 4)
    relays = (w == 1) | (w == 6)
    relay = h * TW + jnp.where(w == 3, 1, 6)
    beyond = h * TW + jnp.where(w == 1, 4, 3)
    beyond_column = jnp.where(w == 1, 0, 2)
    far_column = jnp.where(w == 3, 2, 0)

    extra = crosses | relays
    barrier = pltpu.get_barrier_semaphore()

    def greet(head, tile):
        pl.semaphore_signal(barrier, inc=1, device_id=place(head, tile), device_id_type=MESH)

    for i in range(1, N):
        greet((pu + i) % N, ps)
    for other in (up, down, left, right):
        greet(u, other)

    @pl.when(odd == 1)
    def _():
        greet(pu, ps)

    @pl.when(extra)
    def _():
        for a, b in ((1, 3), (6, 4)):
            other = h * TW + jnp.where(crosses, a, b)
            greet(u, other)
            greet((u + 4) % N, other)


    def columns(ref, head):
        return ref.at[:, pl.ds(pl.multiple_of(head * HD, HD), HD)]

    def a_dst(x, chunk):
        return qb.at[chunk] if x == 2 else kv.at[1, 1, chunk, x]

    def a_copy(x, to):
        ref = (k_hbm, v_hbm, q_hbm)[x]
        return pltpu.make_async_remote_copy(
            src_ref=columns(ref, to), dst_ref=a_dst(x, pu),
            send_sem=a_send.at[x, to], recv_sem=a_recv.at[x, pu],
            device_id=place(to, ps), device_id_type=MESH)

    def a_own(x):
        ref = (k_hbm, v_hbm, q_hbm)[x]
        return pltpu.make_async_copy(columns(ref, u), a_dst(x, u), a_recv.at[x, u])

    def live_copy():
        return pltpu.make_async_remote_copy(
            src_ref=live_hbm, dst_ref=live_in, send_sem=l_send, recv_sem=l_recv,
            device_id=place(pu, ps), device_id_type=MESH)

    def live_own():
        return pltpu.make_async_copy(live_hbm, live_in, l_recv)

    @pl.when(even)
    def _():
        for x in (0, 1, 2):
            a_own(x).start()
        live_own().start()

    def zero(*at):
        @pl.loop(0, N)
        def _(g):
            for part in range(2):
                kv[(*at, g, part)] = jnp.zeros((2 * TILE, HD), jnp.bfloat16)

    for missing, spots in (
        (h == 0, [(c, 0) for c in range(3)]),
        (h == TH - 1, [(c, 2) for c in range(3)]),
        (w == 0, [(0, r) for r in range(3)]),
        (w == TW - 1, [(2, r) for r in range(3)]),
    ):
        @pl.when(missing)
        def _():
            for spot in spots:
                zero(*spot)

    pl.semaphore_wait(barrier, N + 3 + odd + 4 * extra.astype(jnp.int32))

    @pl.when(odd == 1)
    def _():
        for x in (0, 1):
            a_copy(x, pu).start()

    for xs in ((0, 1), (2,)):
        @pl.loop(1, N)
        def _(i):
            to = (pu + N - i) % N
            for x in xs:
                a_copy(x, to).start()

    @pl.when(odd == 1)
    def _():
        a_copy(2, pu).start()
        live_copy().start()

    def v_copy(d, chunk):
        return pltpu.make_async_remote_copy(
            src_ref=kv.at[1, 1, chunk], dst_ref=kv.at[1, 0 if d == 0 else 2, chunk],
            send_sem=v_send.at[d, chunk], recv_sem=v_recv.at[d, chunk],
            device_id=place(u, up if d == 0 else down), device_id_type=MESH)

    def h_copy(d, r, chunk):
        return pltpu.make_async_remote_copy(
            src_ref=kv.at[1, r, chunk], dst_ref=kv.at[0 if d == 0 else 2, r, chunk],
            send_sem=h_send.at[d, r, chunk], recv_sem=h_recv.at[d, r, chunk],
            device_id=place(u, right if d == 0 else left), device_id_type=MESH)

    def near_half(d, r, chunk):
        return pltpu.make_async_remote_copy(
            src_ref=kv.at[1, r, chunk, 0], dst_ref=kv.at[0 if d == 0 else 2, r, chunk, 0],
            send_sem=h_send.at[d, r, chunk], recv_sem=h_recv.at[d, r, chunk],
            device_id=place(u, right if d == 0 else left), device_id_type=MESH)

    def via(chunk):
        return jnp.where(chunk % 2 == 0, u, (u + 4) % N)

    def far_half(r, chunk):
        return pltpu.make_async_remote_copy(
            src_ref=kv.at[1, r, chunk, 1], dst_ref=passing.at[r, chunk],
            send_sem=c_send.at[r, chunk], recv_sem=r_recv.at[r, chunk],
            device_id=place(via(chunk), relay), device_id_type=MESH)

    def forward(r, chunk):
        return pltpu.make_async_remote_copy(
            src_ref=passing.at[r, chunk], dst_ref=kv.at[beyond_column, r, chunk, 1],
            send_sem=r_send.at[r, chunk], recv_sem=c_recv.at[r, chunk],
            device_id=place(via(chunk), beyond), device_id_type=MESH)

    def far_arrival(r, chunk):
        return pltpu.make_async_remote_copy(
            src_ref=passing.at[r, chunk], dst_ref=kv.at[far_column, r, chunk, 1],
            send_sem=r_send.at[r, chunk], recv_sem=c_recv.at[r, chunk],
            device_id=place(via(chunk), beyond), device_id_type=MESH)

    def late(chunk):
        return (chunk + N - u) % N >= N - DIRECT

    def late_by(chunk):
        return (chunk + N - via(chunk)) % N >= N - DIRECT

    def h_start(r, chunk):
        for d, there, wide in ((0, has_right, (w == 3) & ~late(chunk)), (1, has_left, (w == 4) & ~late(chunk))):
            @pl.when(there & ~wide)
            def _():
                h_copy(d, r, chunk).start()

            @pl.when(wide)
            def _():
                far_half(r, chunk).start()
                near_half(d, r, chunk).start()

    def h_arrive(r, chunk):
        for d, there, wide in ((0, has_left, (w == 4) & ~late(chunk)), (1, has_right, (w == 3) & ~late(chunk))):
            @pl.when(there & ~wide)
            def _():
                h_copy(d, r, chunk).wait_recv()

            @pl.when(wide)
            def _():
                near_half(d, r, chunk).wait_recv()
                far_arrival(r, chunk).wait_recv()

    def h_sent(r, chunk):
        for d, there, wide in ((0, has_right, (w == 3) & ~late(chunk)), (1, has_left, (w == 4) & ~late(chunk))):
            @pl.when(there & ~wide)
            def _():
                h_copy(d, r, chunk).wait_send()

            @pl.when(wide)
            def _():
                far_half(r, chunk).wait_send()
                near_half(d, r, chunk).wait_send()

        @pl.when(relays & ~late_by(chunk))
        def _():
            forward(r, chunk).wait_send()

    def rows(action, chunk, which=(0, 1, 2)):
        for r in which:
            if r == 1:
                action(r, chunk)
            else:
                pl.when(has_row[r])(functools.partial(action, r, chunk))

    def pass_on(r, chunk):
        @pl.when(relays & ~late_by(chunk))
        def _():
            far_half(r, chunk).wait_recv()
            forward(r, chunk).start()

    def o_dst(frame, head):
        return out_hbm.at[pl.ds(pl.multiple_of(frame % 2 * TILE, TILE), TILE),
                          pl.ds(pl.multiple_of(head * HD, HD), HD)]

    def o_copy(frame):
        return pltpu.make_async_remote_copy(
            src_ref=ob.at[frame], dst_ref=o_dst(frame, u),
            send_sem=o_send.at[frame], recv_sem=o_recv.at[u, frame % 2],
            device_id=(frame // 2, s), device_id_type=MESH)

    def o_own(frame):
        return pltpu.make_async_copy(ob.at[frame], o_dst(frame, u), o_send.at[frame])

    def attend(f):
        q = qb[f // 2, pl.ds(pl.multiple_of(f % 2 * TILE, TILE), TILE), :]
        spots = []
        for a in range(3):
            g = (f + a + FRAMES - 1) % FRAMES
            spots.append((g // 2, pl.multiple_of(g % 2 * TILE, TILE)))

        def near(c, r, part):
            return jnp.concatenate(
                [kv[c, r, g, part, pl.ds(off, TILE), :] for g, off in spots], axis=0)

        top = jnp.full((TILE, TILE), NEG, jnp.float32)
        for r in range(3):
            for c in range(3):
                scores = lax.dot_general(
                    q, near(c, r, 0), (((1,), (1,)), ((), ())),
                    preferred_element_type=jnp.float32)
                for a in range(3):
                    bias = jnp.where(live[0, f, 0, 9 * a + 3 * r + c] > 0, 0.0, NEG)
                    part = scores[:, a * TILE:(a + 1) * TILE] * LOGIT + bias
                    sc[3 * r + c, :, a * TILE:(a + 1) * TILE] = part
                    top = jnp.maximum(top, part)
        top = jnp.max(top, axis=1, keepdims=True)
        total = jnp.zeros((TILE, TILE), jnp.float32)
        mixed = jnp.zeros((TILE, HD), jnp.float32)
        for r in range(3):
            for c in range(3):
                weights = jnp.exp2(sc[3 * r + c] - top)
                for a in range(3):
                    total += weights[:, a * TILE:(a + 1) * TILE]
                mixed += jnp.dot(
                    weights.astype(jnp.bfloat16), near(c, r, 1),
                    preferred_element_type=jnp.float32)
        ob[f] = (mixed / jnp.sum(total, axis=1, keepdims=True)).astype(jnp.bfloat16)

    def attend_and_send(f):
        attend(f)

        @pl.when(even & (f // 2 == u))
        def _():
            o_own(f).start()

        @pl.when((odd == 1) | (f // 2 != u))
        def _():
            o_copy(f).start()

    def unit(c):
        @pl.loop(0, 2)
        def _(j):
            attend_and_send((2 * c + j + FRAMES - 1) % FRAMES)

    def wait_a(x, chunk):
        pltpu.make_async_copy(columns(k_hbm, 0), a_dst(x, chunk), a_recv.at[x, chunk]).wait()

    @pl.loop(0, N + LAG_H)
    def _(i):
        @pl.when(i < N)
        def _():
            c = (u + i) % N
            wait_a(0, c)
            wait_a(1, c)

            h_start(1, c)

            @pl.when(has_up)
            def _():
                v_copy(0, c).start()

            @pl.when(has_down)
            def _():
                v_copy(1, c).start()

        @pl.when((i >= LAG_V) & (i < N + LAG_V))
        def _():
            c = (u + i + N - LAG_V) % N
            for d, r, there in ((0, 0, has_down), (1, 2, has_up)):
                @pl.when(there)
                def _():
                    v_copy(d, c).wait_recv()
                    h_start(r, c)

        @pl.when((i >= LAG_R) & (i < N + LAG_R))
        def _():
            c = (u + i + N - LAG_R) % N
            rows(pass_on, jnp.where(c % 2 == 0, c, (c + 4) % N), (1, 0, 2))

        @pl.when(i == LAG_H)
        def _():
            live_own().wait()
            pltpu.sync_copy(live_in, live)

        @pl.when(i >= LAG_H)
        def _():
            c = (u + i + N - LAG_H) % N
            rows(h_arrive, c)
            wait_a(2, c)

            @pl.when(i > LAG_H)
            def _():
                unit(c)

    unit(u)

    @pl.when(odd == 1)
    def _():
        live_copy().wait_send()

    @pl.loop(0, N)
    def _(g):
        @pl.when(has_up)
        def _():
            v_copy(0, g).wait_send()

        @pl.when(has_down)
        def _():
            v_copy(1, g).wait_send()

        rows(h_sent, g)

        @pl.when((odd == 1) | (g != u))
        def _():
            for x in range(3):
                a_copy(x, g).wait_send()
            for j in range(2):
                o_copy(2 * g + j).wait_send()
                pltpu.make_async_copy(ob.at[j], o_dst(j, g), o_recv.at[g, j]).wait()

        @pl.when(even & (g == u))
        def _():
            for j in range(2):
                o_own(2 * g + j).wait()


def local(query, key, value, live):
    rows, width = query.shape
    hbm = pl.BlockSpec(memory_space=pl.ANY)
    return pl.pallas_call(
        kernel,
        out_shape=jax.ShapeDtypeStruct((rows, width), jnp.bfloat16),
        in_specs=[hbm] * 4,
        out_specs=hbm,
        scratch_shapes=[
            pltpu.VMEM((3, 3, N, 2, 2 * TILE, HD), jnp.bfloat16),
            pltpu.VMEM((N, 2 * TILE, HD), jnp.bfloat16),
            pltpu.VMEM((FRAMES, TILE, HD), jnp.bfloat16),
            pltpu.VMEM((9, TILE, 3 * TILE), jnp.float32),
            pltpu.VMEM((3, N, 2 * TILE, HD), jnp.bfloat16),
            pltpu.VMEM(live.shape, jnp.int32), pltpu.SMEM(live.shape, jnp.int32),
            DMA((3, N)), DMA((3, N)),
            DMA((2, N)), DMA((2, N)),
            DMA((2, 3, N)), DMA((2, 3, N)),
            DMA((3, N)), DMA((3, N)), DMA((3, N)), DMA((3, N)),
            DMA((FRAMES,)), DMA((N, 2)),
            DMA, DMA,
        ],
        compiler_params=pltpu.CompilerParams(
            collective_id=0, has_side_effects=True, vmem_limit_bytes=53 << 20),
    )(query, key, value, live)


def solution(mesh):
    return jax.shard_map(
        local,
        mesh=mesh,
        in_specs=(
            P(("uly", "blk"), None),
            P(("uly", "blk"), None),
            P(("uly", "blk"), None),
            P("uly", None, "blk", None),
        ),
        out_specs=P(("uly", "blk"), None),
        check_vma=False,
    )
```
